32 devices in a mesh: section: 2 (over core), seq: 4 (over z), fsdp: 4 (over y, x).
Axes of the slice: x: 2, y: 2, z: 4, core: 2. Of those that a mesh axis runs over, the one named last changes fastest.
Arguments:
- inputs: float32 [2, 4, 512, 768], P(None, 'fsdp', 'seq'), may hold values from -6 to 6
- out_grad: float32 [2, 4, 512, 768], P(None, 'fsdp', 'seq'), may hold values from -6 to 6
- norm_gain: bfloat16 [2, 768], P('section', 'fsdp'), may hold values from 0.099609375 to 1.8984375
- input_weight: bfloat16 [2, 768, 3328], P('section', 'fsdp'), may hold values from -0.21875 to 0.21875
- conv_weight: bfloat16 [2, 4, 1792], P('section', None, 'fsdp'), may hold values from -3 to 3
- conv_bias: bfloat16 [2, 1792], P('section', 'fsdp'), may hold values from -3 to 3
- skip_gain: bfloat16 [2, 24], P('section', 'fsdp'), may hold values from 1 to 4
- gate_gain: bfloat16 [2, 1536], P('section', 'fsdp'), may hold values from 0.099609375 to 1.8984375
- out_weight: bfloat16 [2, 1536, 768], P('section', 'fsdp'), may hold values from -0.15625 to 0.15625
- step_codes: int32 [2, 2, 4, 512, 24], P('section', None, 'fsdp', 'seq'), may hold values from 128 to 512
- decay_codes: int32 [2, 2, 4, 512, 24], P('section', None, 'fsdp', 'seq'), may hold values from 2 to 45000, as said below
Outputs:
- section_outputs: float32 [2, 2, 4, 512, 768], P('section', None, 'fsdp', 'seq')
- section_input_grads: float32 [2, 2, 4, 512, 768], P('section', None, 'fsdp', 'seq')
- norm_gain_grad: float32 [2, 768], P('section', 'fsdp')
- in_weight_grad: float32 [2, 768, 3328], P('section', 'fsdp')
- conv_weight_grad: float32 [2, 4, 1792], P('section', None, 'fsdp')
- conv_bias_grad: float32 [2, 1792], P('section', 'fsdp')
- skip_gain_grad: float32 [2, 24], P('section', 'fsdp')
- gate_gain_grad: float32 [2, 1536], P('section', 'fsdp')
- out_weight_grad: float32 [2, 1536, 768], P('section', 'fsdp')
The draws below stay inside these ranges and needn't reach their ends.
Inputs may be any that keep to these rules, and one draw needn't show every extreme that they name: `decay_codes`: codes are positive.
All inputs are finite; a program needn't handle non-finite values.
Results may differ from the reference program's by a relative error of at most 0.012.
Values may be sent and summed in bfloat16 or wider, within the bound.
A program may use at most 256 MiB of HBM per device.

```python
import math
from functools import partial
import jax
import jax.numpy as jnp
from jax import lax

D = 768
DI = 1536
HEADS = 24
HEAD_DIM = 64
STATE = 128
CONV = 4
MICRO = 2
TOK_DEV = 128
LAYERS = 2
SEQS = 4
L = 512
PROJ = 3328
DC = 1792


def draw_decay_codes(key, part):
    subkeys = jax.random.split(key, 7)
    blocks = L // TOK_DEV
    fast_heads = jax.random.randint(subkeys[0], (LAYERS, 1, 1, 1, 1, HEADS), 0, 5) < 2
    fast_base = jax.random.randint(subkeys[1], (LAYERS, 1, 1, 1, 1, HEADS), 1300, 2200)
    slow_base = jax.random.randint(subkeys[2], (LAYERS, 1, 1, 1, 1, HEADS), 2, 5)
    head_base = jnp.where(fast_heads, fast_base, slow_base)
    device_factor = jax.random.randint(subkeys[3], (LAYERS, MICRO, SEQS, blocks, 1, HEADS), 2, 6)
    token_factor = jax.random.randint(subkeys[4], (LAYERS, MICRO, SEQS, blocks, TOK_DEV, HEADS), 2, 5)
    attenuation_multipliers = head_base * device_factor * token_factor // 4
    attenuation_multipliers = attenuation_multipliers.reshape(LAYERS, MICRO, SEQS, L, HEADS)
    location_series = jax.random.randint(subkeys[5], (LAYERS, MICRO, SEQS, 1, 3), 0, L)
    drawn = jax.random.randint(subkeys[6], (LAYERS, MICRO, SEQS, 1, 3), 15000, 45000)
    which = lax.broadcasted_iota(jnp.int32, (LAYERS, MICRO, SEQS, 1, 3), 4)
    quantity_series = jnp.where(which == 0, 45000, drawn)
    sequence_indices = lax.broadcasted_iota(jnp.int32, (LAYERS, MICRO, SEQS, L, 3), 3)
    clustered_sets = jnp.max(jnp.where(sequence_indices == location_series, quantity_series, 0), axis=-1)
    return jnp.maximum(attenuation_multipliers, clustered_sets[..., None]).astype(jnp.int32)


def plant(values, own_key, least, top_value):
    longest = values.shape.index(max(values.shape))
    spots = []
    for shift in (0, 1):
        where = [jax.random.randint(jax.random.fold_in(own_key, axis), (), 0, length) for axis, length in enumerate(values.shape)]
        where[longest] = (where[longest] + shift) % values.shape[longest]
        spots.append(tuple(where))
    return values.at[spots[0]].set(least).at[spots[1]].set(top_value)


def steps_of(stream_key, shape, cuts, least, high):
    level, own = 1.0, jax.random.fold_in(stream_key, 6)
    for axis_at, blocks in cuts:
        draws = jnp.exp(jax.random.uniform(jax.random.fold_in(own, axis_at), (blocks,), jnp.float32, least / len(cuts), high / len(cuts)))
        level = level * jnp.repeat(draws, shape[axis_at] // blocks).reshape([-1 if axis == axis_at else 1 for axis in range(len(shape))])
    return level


def scatter_about(stream_key, dims, spread, bound, cuts=(), dtype=jnp.bfloat16):
    level = steps_of(stream_key, dims, cuts, -0.22, 0.18) if cuts else 1.0
    values = jax.random.normal(stream_key, dims, jnp.float32) * spread * level
    return jnp.minimum(jnp.maximum(values, -bound), bound).astype(dtype)


def setup_inputs(seed: int = 0) -> dict:
    splits = jax.random.split(jax.random.key(seed), 12)
    inputs = scatter_about(splits[0], (MICRO, SEQS, L, D), 1.0, 6.0, ((1, 4), (2, 4)), jnp.float32)
    out_grad = scatter_about(splits[1], (MICRO, SEQS, L, D), 1.0, 6.0, ((1, 4), (2, 4)), jnp.float32)
    norm_gain = jnp.clip(1.0 + 0.18 * jax.random.normal(splits[2], (LAYERS, D), jnp.float32), 0.099609375, 1.8984375).astype(jnp.bfloat16)
    input_weight = scatter_about(splits[3], (LAYERS, D, PROJ), D ** -0.5, 0.21875, ((0, 2), (1, 4)))
    conv_weight = scatter_about(splits[4], (LAYERS, CONV, DC), CONV ** -0.5, 3.0, ((0, 2), (2, 4)))
    conv_bias = scatter_about(splits[5], (LAYERS, DC), 0.5, 3.0, ((0, 2), (1, 4)))
    skip_gain = jnp.clip(jnp.exp(math.log(4.0) - 1.3862944 * jax.random.uniform(splits[6], (LAYERS, HEADS), jnp.float32) ** steps_of(splits[6], (LAYERS, HEADS), ((0, 2), (1, 4)), -0.2, 0.2)), 1.0, 4.0).astype(jnp.bfloat16)
    gate_gain = jnp.clip(1.0 + 0.18 * jax.random.normal(splits[7], (LAYERS, DI), jnp.float32), 0.099609375, 1.8984375).astype(jnp.bfloat16)
    out_weight = scatter_about(splits[8], (LAYERS, DI, D), DI ** -0.5, 0.15625, ((0, 2), (1, 4)))
    step_codes = plant(jax.random.randint(splits[9], (LAYERS, MICRO, SEQS, L, HEADS), 128, 513), jax.random.fold_in(splits[9], 1), 128, 512).astype(jnp.int32)
    decay_codes = draw_decay_codes(jax.random.fold_in(splits[11], 71), 0)
    return {"inputs": inputs, "out_grad": out_grad, "norm_gain": norm_gain, "input_weight": input_weight, "conv_weight": conv_weight, "conv_bias": conv_bias, "skip_gain": skip_gain, "gate_gain": gate_gain, "out_weight": out_weight, "step_codes": step_codes, "decay_codes": decay_codes}


EPSILON = 1e-05
STEP_SCALE = 256.0
DECAY_SCALE = 65536.0
HIGHEST = lax.Precision.HIGHEST

def norm_input(hidden, gain_vector):
    inverse_rms = lax.rsqrt(lax.optimization_barrier(jnp.mean(hidden * hidden, axis=-1, keepdims=True)) + EPSILON)
    return hidden * inverse_rms * gain_vector

def gated_norm(mixer_out, gate_outputs, gain_vector):
    gated_products = mixer_out * jax.nn.silu(gate_outputs)
    inverse_rms = lax.rsqrt(lax.optimization_barrier(jnp.mean(gated_products * gated_products, axis=-1, keepdims=True)) + EPSILON)
    return gated_products * inverse_rms * gain_vector

def conv_silu(before, current, kernel, offset):
    extended = jnp.concatenate([before, current], axis=0)
    length = current.shape[0]
    summed = offset[None, :] + kernel[0][None, :] * extended[0:length]
    for shift_row in range(1, kernel.shape[0]):
        summed = summed + kernel[shift_row][None, :] * extended[shift_row:shift_row + length]
    return jax.nn.silu(summed)

def split_mixer(conv_part):
    length = conv_part.shape[0]
    head_values = conv_part[:, :DI].reshape(length, HEADS, HEAD_DIM)
    input_keys = conv_part[:, DI:DI + STATE]
    output_queries = conv_part[:, DI + STATE:]
    return (head_values, input_keys, output_queries)

def step_and_decay(step_block, decay_block):
    step_sizes = step_block.astype(jnp.float32) / STEP_SCALE
    cumulative = jnp.cumsum(-decay_block.astype(jnp.float32) / DECAY_SCALE, axis=0)
    return (step_sizes, cumulative)

def block_summary(head_values, input_keys, step_sizes, cumulative):
    to_end = jnp.exp(cumulative[-1][None, :] - cumulative) * step_sizes
    return jnp.einsum('sh,shp,sn->hpn', to_end, head_values, input_keys, precision=HIGHEST)

def block_output(head_values, input_keys, output_queries, step_sizes, cumulative, entering, skip_weights):
    length = head_values.shape[0]
    later = lax.broadcasted_iota(jnp.int32, (length, length), 0)
    earlier = lax.broadcasted_iota(jnp.int32, (length, length), 1)
    causal = (later >= earlier)[None, :, :]
    cum_heads = cumulative.T
    dispersion_width = cum_heads[:, :, None] - cum_heads[:, None, :]
    decays = jnp.where(causal, jnp.exp(jnp.where(causal, dispersion_width, 0.0)), 0.0)
    scores = jnp.dot(output_queries, input_keys.T, precision=HIGHEST)
    coupling = decays * scores[None, :, :] * step_sizes.T[:, None, :]
    within = jnp.einsum('hts,shp->thp', coupling, head_values, precision=HIGHEST)
    carried = jnp.exp(cumulative)[:, :, None] * jnp.einsum('tn,hpn->thp', output_queries, entering, precision=HIGHEST)
    return within + carried + skip_weights[None, :, None] * head_values

def mixer_blocks(head_values, input_keys, output_queries, skip_weights, step_sizes, cumulative, entering):
    mixed = jax.vmap(block_output, in_axes=(0, 0, 0, 0, 0, 0, None))(head_values, input_keys, output_queries, step_sizes, cumulative, entering, skip_weights)
    summaries = jax.vmap(block_summary)(head_values, input_keys, step_sizes, cumulative)
    return (mixed, summaries)

def sequence_parts(hidden, params, step_rows, decay_rows):
    normed = norm_input(hidden, params[1].astype(jnp.float32)).astype(jnp.bfloat16)
    projected = jnp.dot(normed, params[0], preferred_element_type=jnp.float32)
    gate_outputs = projected[:, :DI]
    mixer_rows = projected[:, DI:]
    before = jnp.zeros((CONV - 1, mixer_rows.shape[1]), jnp.float32)
    conv_part = conv_silu(before, mixer_rows, params[2].astype(jnp.float32), params[3].astype(jnp.float32))
    blocks = hidden.shape[0] // TOK_DEV
    head_values, input_keys, output_queries = split_mixer(conv_part)
    head_values = head_values.reshape(blocks, TOK_DEV, HEADS, HEAD_DIM)
    input_keys = input_keys.reshape(blocks, TOK_DEV, STATE)
    output_queries = output_queries.reshape(blocks, TOK_DEV, STATE)
    step_sizes, cumulative = jax.vmap(step_and_decay)(step_rows.reshape(blocks, TOK_DEV, HEADS), decay_rows.reshape(blocks, TOK_DEV, HEADS))
    summaries = jax.vmap(block_summary)(head_values, input_keys, step_sizes, cumulative)

    def advance(state_now, pieces):
        return (jnp.exp(pieces[0])[:, None, None] * state_now + pieces[1], state_now)
    _, entering = lax.scan(advance, jnp.zeros(summaries.shape[1:], jnp.float32), (cumulative[:, -1], summaries))
    return (normed, gate_outputs, mixer_rows, before, head_values, input_keys, output_queries, step_sizes, cumulative, entering)

def forward_sequence(params, sequence_item):
    hidden, step_rows, decay_rows = sequence_item
    parts = sequence_parts(hidden, params, step_rows, decay_rows)
    normed, gate_outputs, mixer_rows, before, head_values, input_keys, output_queries, step_sizes, cumulative, entering = parts
    mixed, _ = mixer_blocks(head_values, input_keys, output_queries, params[4].astype(jnp.float32), step_sizes, cumulative, entering)
    mixer_out = mixed.reshape(hidden.shape[0], DI)
    normed_out = gated_norm(mixer_out, gate_outputs, params[5].astype(jnp.float32)).astype(jnp.bfloat16)
    return hidden + jnp.dot(normed_out, params[6], preferred_element_type=jnp.float32)

def backward_sequence(params, sequence_item):
    hidden, out_cot, step_rows, decay_rows = sequence_item
    length = hidden.shape[0]
    parts = sequence_parts(hidden, params, step_rows, decay_rows)
    normed, gate_outputs, mixer_rows, before, head_values, input_keys, output_queries, step_sizes, cumulative, entering = parts

    def mixer_fn(values_in, keys_in, queries_in, skip_in):
        return mixer_blocks(values_in, keys_in, queries_in, skip_in, step_sizes, cumulative, entering)
    (mixed, _), mixer_vjp = jax.vjp(mixer_fn, head_values, input_keys, output_queries, params[4].astype(jnp.float32))
    mixer_out = mixed.reshape(length, DI)
    normed_out, norm_vjp = jax.vjp(gated_norm, mixer_out, gate_outputs, params[5].astype(jnp.float32))
    out_rounded = normed_out.astype(jnp.bfloat16)
    cot_rounded = out_cot.astype(jnp.bfloat16)
    grad_out_weight = jnp.dot(out_rounded.T, cot_rounded, preferred_element_type=jnp.float32)
    grad_normed_out = jnp.dot(cot_rounded, params[6].T, preferred_element_type=jnp.float32)
    grad_mixer, grad_gate, grad_gate_gain = norm_vjp(grad_normed_out)
    grad_heads = grad_mixer.reshape(head_values.shape)
    local_entry = jnp.einsum('bth,bthp,btn->bhpn', jnp.exp(cumulative), grad_heads, output_queries, precision=HIGHEST)

    def retreat(carry_grad, pieces):
        return (pieces[1] + jnp.exp(pieces[0])[:, None, None] * carry_grad, carry_grad)
    _, leaving = lax.scan(retreat, jnp.zeros(local_entry.shape[1:], jnp.float32), (cumulative[:, -1], local_entry), reverse=True)
    grad_values, grad_keys, grad_queries, grad_skip = mixer_vjp((grad_heads, leaving))
    grad_conv = jnp.concatenate([grad_values.reshape(length, DI), grad_keys.reshape(length, STATE), grad_queries.reshape(length, STATE)], axis=1)

    def conv_fn(rows_in, kernel_in, offset_in):
        return conv_silu(before, rows_in, kernel_in, offset_in)
    _, conv_vjp = jax.vjp(conv_fn, mixer_rows, params[2].astype(jnp.float32), params[3].astype(jnp.float32))
    grad_rows, grad_kernel, grad_offset = conv_vjp(grad_conv)
    grad_projected = jnp.concatenate([grad_gate, grad_rows], axis=1).astype(jnp.bfloat16)
    grad_in_weight = jnp.dot(normed.T, grad_projected, preferred_element_type=jnp.float32)
    grad_normed = jnp.dot(grad_projected, params[0].T, preferred_element_type=jnp.float32)
    _, input_vjp = jax.vjp(norm_input, hidden, params[1].astype(jnp.float32))
    grad_hidden, grad_norm_gain = input_vjp(grad_normed)
    pieces = (grad_in_weight, grad_norm_gain, grad_kernel, grad_offset, grad_skip, grad_gate_gain, grad_out_weight)
    return (out_cot + grad_hidden, pieces)

def accumulate(params, totals, sequence_item):
    grad_hidden, pieces = backward_sequence(params, sequence_item)
    return (tuple((running + added for running, added in zip(totals, pieces))), grad_hidden)

def reference(inputs, out_grad, norm_gain, input_weight, conv_weight, conv_bias, skip_gain, gate_gain, out_weight, step_codes, decay_codes):
    sequences = inputs.shape[0] * inputs.shape[1]
    length = inputs.shape[2]
    current = inputs.reshape(sequences, length, D)
    layer_inputs = []
    layer_outputs = []
    all_params = []
    for layer_index in range(LAYERS):
        params = (input_weight[layer_index], norm_gain[layer_index], conv_weight[layer_index], conv_bias[layer_index], skip_gain[layer_index], gate_gain[layer_index], out_weight[layer_index])
        all_params.append(params)
        step_rows = step_codes[layer_index].reshape(sequences, length, HEADS)
        decay_rows = decay_codes[layer_index].reshape(sequences, length, HEADS)
        layer_inputs.append(current)
        current = lax.map(partial(forward_sequence, params), (current, step_rows, decay_rows))
        layer_outputs.append(current)
    adjoint_vector = out_grad.reshape(sequences, length, D)
    input_grads = [None] * LAYERS
    weight_grads = [None] * LAYERS
    for layer_index in range(LAYERS - 1, -1, -1):
        params = all_params[layer_index]
        step_rows = step_codes[layer_index].reshape(sequences, length, HEADS)
        decay_rows = decay_codes[layer_index].reshape(sequences, length, HEADS)
        zero_totals = tuple((jnp.zeros(weight.shape, jnp.float32) for weight in params))
        totals, adjoint_vector = lax.scan(partial(accumulate, params), zero_totals, (layer_inputs[layer_index], adjoint_vector, step_rows, decay_rows))
        input_grads[layer_index] = adjoint_vector
        weight_grads[layer_index] = totals
    shape_out = (LAYERS, MICRO, SEQS, length, D)
    section_outputs = jnp.stack(layer_outputs).reshape(shape_out)
    section_input_grads = jnp.stack(input_grads).reshape(shape_out)
    stacked = [jnp.stack([weight_grads[layer_index][member] for layer_index in range(LAYERS)]) for member in range(7)]
    return (section_outputs, section_input_grads, stacked[1], stacked[0], stacked[2], stacked[3], stacked[4], stacked[5], stacked[6])
```

```python
import jax
import jax.numpy as jnp
from jax import lax
from jax.sharding import PartitionSpec as P

DI = 1536
HEADS = 24
HEAD_DIM = 64
STATE = 128
CONV = 4


EPSILON = 1e-05
STEP_SCALE = 256.0
DECAY_SCALE = 65536.0
HIGHEST = lax.Precision.HIGHEST


def passed_along(x, axis, by):
    size = lax.axis_size(axis)
    pairs = [(i, i + by) for i in range(size) if 0 <= i + by < size]
    return lax.ppermute(x, axis, pairs)


def carried_in(local, totals, backward):
    count, mine = (lax.axis_size("seq"), lax.axis_index("seq"))
    pieces = lax.all_gather(local.astype(jnp.bfloat16), "seq")
    source = lax.broadcasted_iota(jnp.int32, (count, count), 0)
    between = lax.broadcasted_iota(jnp.int32, (count, count), 1)
    if backward:
        inside = (between > mine) & (between < source)
        used = jnp.arange(count) > mine
    else:
        inside = (between > source) & (between < mine)
        used = jnp.arange(count) < mine
    decay = jnp.sum(jnp.where(inside[:, :, None], totals[None], 0.0), axis=1)
    weight = jnp.where(used[:, None], jnp.exp(decay), 0.0)
    return jnp.sum(weight[:, :, None, None] * pieces.astype(jnp.float32), axis=0)


def norm_input(hidden, gain_vector):
    inverse_rms = lax.rsqrt(jnp.mean(hidden * hidden, axis=-1, keepdims=True) + EPSILON)
    return hidden * inverse_rms * gain_vector


def gated_norm(mixer_out, gate_outputs, gain_vector):
    gated_products = mixer_out * jax.nn.silu(gate_outputs)
    inverse_rms = lax.rsqrt(
        jnp.mean(gated_products * gated_products, axis=-1, keepdims=True) + EPSILON
    )
    return gated_products * inverse_rms * gain_vector


def conv_silu(before, current, kernel, offset):
    extended = jnp.concatenate([before, current], axis=0)
    length = current.shape[0]
    summed = offset[None, :] + kernel[0][None, :] * extended[0:length]
    for shift_row in range(1, kernel.shape[0]):
        summed = summed + kernel[shift_row][None, :] * extended[shift_row : shift_row + length]
    return jax.nn.silu(summed)


def split_mixer(conv_part):
    length = conv_part.shape[0]
    head_values = conv_part[:, :DI].reshape(length, HEADS, HEAD_DIM)
    input_keys = conv_part[:, DI : DI + STATE]
    output_queries = conv_part[:, DI + STATE :]
    return (head_values, input_keys, output_queries)


def block_summary(head_values, input_keys, step_sizes, cumulative):
    to_end = jnp.exp(cumulative[-1][None, :] - cumulative) * step_sizes
    return jnp.einsum("sh,shp,sn->hpn", to_end, head_values, input_keys, precision=HIGHEST)


def block_output(
    head_values, input_keys, output_queries, step_sizes, cumulative, entering, skip_weights
):
    length = head_values.shape[0]
    later = lax.broadcasted_iota(jnp.int32, (length, length), 0)
    earlier = lax.broadcasted_iota(jnp.int32, (length, length), 1)
    causal = (later >= earlier)[None, :, :]
    cum_heads = cumulative.T
    dispersion_width = cum_heads[:, :, None] - cum_heads[:, None, :]
    decays = jnp.where(causal, jnp.exp(jnp.where(causal, dispersion_width, 0.0)), 0.0)
    scores = jnp.dot(output_queries, input_keys.T, precision=HIGHEST)
    coupling = decays * scores[None, :, :] * step_sizes.T[:, None, :]
    within = jnp.einsum("hts,shp->thp", coupling, head_values, precision=HIGHEST)
    carried = jnp.exp(cumulative)[:, :, None] * jnp.einsum(
        "tn,hpn->thp", output_queries, entering, precision=HIGHEST
    )
    return within + carried + skip_weights[None, :, None] * head_values


def front_part(hidden, params):
    normed = norm_input(hidden, params[1].astype(jnp.float32)).astype(jnp.bfloat16)
    projected = jnp.dot(normed, params[0], preferred_element_type=jnp.float32)
    return (normed, projected[:, :DI], projected[:, DI:])


def layer_forward(hidden, params, step_sizes, cumulative, totals):
    normed, gate_outputs, mixer_rows = front_part(hidden, params)
    before = passed_along(mixer_rows[-(CONV - 1) :], "seq", 1)
    conv_part = conv_silu(
        before, mixer_rows, params[2].astype(jnp.float32), params[3].astype(jnp.float32)
    )
    head_values, input_keys, output_queries = split_mixer(conv_part)
    summary = block_summary(head_values, input_keys, step_sizes, cumulative)
    entering = carried_in(summary, totals, False)
    mixed = block_output(
        head_values,
        input_keys,
        output_queries,
        step_sizes,
        cumulative,
        entering,
        params[4].astype(jnp.float32),
    )
    mixer_out = mixed.reshape(hidden.shape[0], DI)
    normed_out = gated_norm(mixer_out, gate_outputs, params[5].astype(jnp.float32)).astype(
        jnp.bfloat16
    )
    result = hidden + jnp.dot(normed_out, params[6], preferred_element_type=jnp.float32)
    return (result, before, entering)


def layer_backward(
    hidden, before, entering, step_sizes, cumulative, totals, out_cot, params
):
    length = hidden.shape[0]
    normed, gate_outputs, mixer_rows = front_part(hidden, params)
    kernel = params[2].astype(jnp.float32)
    offset = params[3].astype(jnp.float32)
    conv_part, conv_vjp = jax.vjp(conv_silu, before, mixer_rows, kernel, offset)
    head_values, input_keys, output_queries = split_mixer(conv_part)

    def mixer_fn(values_in, keys_in, queries_in, skip_in):
        mixed_here = block_output(
            values_in, keys_in, queries_in, step_sizes, cumulative, entering, skip_in
        )
        return (mixed_here, block_summary(values_in, keys_in, step_sizes, cumulative))

    (mixed, _), mixer_vjp = jax.vjp(
        mixer_fn, head_values, input_keys, output_queries, params[4].astype(jnp.float32)
    )
    mixer_out = mixed.reshape(length, DI)
    normed_out, norm_vjp = jax.vjp(
        gated_norm, mixer_out, gate_outputs, params[5].astype(jnp.float32)
    )
    out_rounded = normed_out.astype(jnp.bfloat16)
    cot_rounded = out_cot.astype(jnp.bfloat16)
    grad_normed_out = jnp.dot(cot_rounded, params[6].T, preferred_element_type=jnp.float32)
    grad_mixer, grad_gate, grad_gate_gain = norm_vjp(grad_normed_out)
    grad_heads = grad_mixer.reshape(length, HEADS, HEAD_DIM)
    local_entry = jnp.einsum(
        "th,thp,tn->hpn", jnp.exp(cumulative), grad_heads, output_queries, precision=HIGHEST
    )
    leaving = carried_in(local_entry, totals, True)
    grad_values, grad_keys, grad_queries, grad_skip = mixer_vjp((grad_heads, leaving))
    grad_conv = jnp.concatenate([grad_values.reshape(length, DI), grad_keys, grad_queries], axis=1)
    grad_before, grad_rows, grad_kernel, grad_offset = conv_vjp(grad_conv)
    upstream_adjoint = passed_along(grad_before, "seq", -1)
    grad_rows = grad_rows.at[-(CONV - 1) :].add(upstream_adjoint)
    grad_projected = jnp.concatenate([grad_gate, grad_rows], axis=1).astype(jnp.bfloat16)
    grad_normed = jnp.dot(grad_projected, params[0].T, preferred_element_type=jnp.float32)
    _, input_vjp = jax.vjp(norm_input, hidden, params[1].astype(jnp.float32))
    grad_hidden, grad_norm_gain = input_vjp(grad_normed)
    smalls = (grad_norm_gain, grad_kernel, grad_offset, grad_skip, grad_gate_gain)
    factors = (normed, grad_projected, out_rounded, cot_rounded)
    return (out_cot + grad_hidden, smalls, factors)


def packed(parts):
    flat = jnp.concatenate([part.reshape(-1) for part in parts])
    return jnp.pad(flat, (0, -flat.size % 1024))


def swapped(x):
    return lax.ppermute(x, "section", [(0, 1), (1, 0)])


def body(
    inputs,
    out_grad,
    norm_gain,
    input_weight,
    conv_weight,
    conv_bias,
    skip_gain,
    gate_gain,
    out_weight,
    step_codes,
    decay_codes,
):
    section = lax.axis_index("section")
    first = section == 0
    layers = lax.axis_size("section")
    owners = lax.axis_size("fsdp")
    assert layers == 2 and inputs.shape[0] == 2

    def by_layer(mine, theirs):
        return (jnp.where(first, mine, theirs), jnp.where(first, theirs, mine))

    def both_layers(shard):
        rows = shard.shape[0] // layers
        kept = lax.dynamic_slice_in_dim(shard, section * rows, rows, 0)
        sent = lax.dynamic_slice_in_dim(shard, (1 - section) * rows, rows, 0)
        return [
            lax.all_gather(half, ("fsdp", "section"), axis=0, tiled=True)
            for half in by_layer(kept, swapped(sent))
        ]

    in_weights = both_layers(input_weight[0])
    out_weights = both_layers(out_weight[0])
    small_shards = (norm_gain[0], conv_weight[0], conv_bias[0], skip_gain[0], gate_gain[0])
    small_rows = lax.all_gather(packed(small_shards), ("section", "fsdp"))
    small_rows = small_rows.reshape(layers, owners, -1)
    params = []
    for layer in range(layers):
        smalls, at = [], 0
        for shard in small_shards:
            part = small_rows[layer, :, at : at + shard.size].reshape((owners,) + shard.shape)
            at += shard.size
            part = jnp.moveaxis(part, 0, -2)
            smalls.append(part.reshape(part.shape[:-2] + (-1,)))
        params.append((in_weights[layer], *smalls, out_weights[layer]))

    codes = jnp.stack([step_codes[0, :, 0], decay_codes[0, :, 0]], axis=1).astype(jnp.float32)
    here = jnp.where(first, codes[0], codes[1])
    there = jnp.where(first, codes[1], codes[0])
    codes = by_layer(here, swapped(there))
    steps = [code[0] / STEP_SCALE for code in codes]
    cumulatives = [jnp.cumsum(-code[1] / DECAY_SCALE, axis=0) for code in codes]
    totals = lax.all_gather(jnp.stack([part[-1] for part in cumulatives]), "seq")

    hidden = jnp.where(first, inputs[0, 0], inputs[1, 0])
    results, kept_values = [], []
    for layer in range(layers):
        result, before, entering = layer_forward(
            hidden, params[layer], steps[layer], cumulatives[layer], totals[:, layer]
        )
        kept_values.append((hidden, before, entering))
        results.append(result)
        hidden = result

    adjoint = jnp.where(first, out_grad[0, 0], out_grad[1, 0])
    gradients, small_sums, factors, received = [None] * 2, [None] * 2, [None] * 2, [None] * 2
    for layer in reversed(range(layers)):
        adjoint, smalls, factor = layer_backward(
            *kept_values[layer],
            steps[layer],
            cumulatives[layer],
            totals[:, layer],
            adjoint,
            params[layer],
        )
        gradients[layer] = adjoint
        small_sums[layer] = packed(smalls)
        factors[layer] = jnp.concatenate(factor, axis=1)
        received[layer] = lax.ppermute(factors[layer], "section", [(1 - layer, layer)])
    rows = jnp.concatenate(
        [jnp.where(first, factors[0], factors[1]), jnp.where(first, received[0], received[1])],
        axis=0,
    )
    width, projection = params[0][0].shape
    normed_rows = rows[:, :width]
    projected_rows = rows[:, width : width + projection]
    output_rows = rows[:, width + projection : width + projection + DI]
    cotangent_rows = rows[:, width + projection + DI :]
    grad_in = jnp.dot(normed_rows.T, projected_rows, preferred_element_type=jnp.float32)
    grad_out = jnp.dot(output_rows.T, cotangent_rows, preferred_element_type=jnp.float32)
    shares = tuple(
        lax.psum_scatter(
            value.astype(jnp.bfloat16), "fsdp", scatter_dimension=0, tiled=True
        )
        for value in (grad_in, grad_out)
    )
    grad_in, grad_out = lax.psum(shares, "seq")

    summed = lax.psum(jnp.stack(small_sums), ("section", "seq", "fsdp"))
    summed = jnp.where(first, summed[0], summed[1])
    owner, at, small_grads = lax.axis_index("fsdp"), 0, []
    for weight in params[0][1:6]:
        whole = summed[at : at + weight.size].reshape(weight.shape)
        at += weight.size
        share = weight.shape[-1] // owners
        small_grads.append(lax.dynamic_slice_in_dim(whole, owner * share, share, -1))

    def owned(values):
        mine = jnp.where(first, values[0], values[1])
        got = swapped(jnp.where(first, values[1], values[0]))
        return jnp.stack(by_layer(mine, got))

    return (
        owned(results)[None, :, None],
        owned(gradients)[None, :, None],
        small_grads[0][None],
        grad_in.astype(jnp.float32)[None],
        small_grads[1][None],
        small_grads[2][None],
        small_grads[3][None],
        small_grads[4][None],
        grad_out.astype(jnp.float32)[None],
    )


def solution(mesh):
    return jax.shard_map(
        body,
        mesh=mesh,
        in_specs=(
            P(None, "fsdp", "seq", None),
            P(None, "fsdp", "seq", None),
            P("section", "fsdp"),
            P("section", "fsdp", None),
            P("section", None, "fsdp"),
            P("section", "fsdp"),
            P("section", "fsdp"),
            P("section", "fsdp"),
            P("section", "fsdp", None),
            P("section", None, "fsdp", "seq", None),
            P("section", None, "fsdp", "seq", None),
        ),
        out_specs=(
            P("section", None, "fsdp", "seq", None),
            P("section", None, "fsdp", "seq", None),
            P("section", "fsdp"),
            P("section", "fsdp", None),
            P("section", None, "fsdp"),
            P("section", "fsdp"),
            P("section", "fsdp"),
            P("section", "fsdp"),
            P("section", "fsdp", None),
        ),
        check_vma=False,
    )
```
